32 devices in a mesh: grp: 2 (over x), row: 16 (over z, y, core).
Axes of the slice: x: 2, y: 2, z: 4, core: 2. Of those that a mesh axis runs over, the one named last changes fastest.
Arguments:
- saved_rows: float32 [32, 512, 32, 128], P(None, None, ('grp', 'row')), may hold values from -3 to 3
- table_order: int32 [32], replicated, may hold values from 0 to 31, each once
- owner_shard: int32 [32, 32, 128, 1], P(None, ('grp', 'row')), may hold values from 0 to 15; in each aligned block of 128 rows (0 to 127, 128 to 255, ..., all dimensions but the last counted through in order) at most 24 rows name the same one
- row_in_shard: int32 [32, 32, 128], P(None, ('grp', 'row')), may hold values from 0 to 1023
- bag_owner: int32 [32, 32, 128], P(None, ('grp', 'row')), may hold values from 0 to 15, never falling along the last dimension, each value on 1 to 32 neighbouring positions
Outputs:
- pooled: float32 [512, 32, 128], P(('grp', 'row'))
The draws below stay inside these ranges and needn't reach their ends.
Inputs may be any that keep to these rules, and one draw needn't show every extreme that they name: `owner_shard`: among the 128 ids of one table and one device, no shard number occurs more than 24 times, and 24 is reached in some of these blocks. `bag_owner`: never falls along the last dimension; every sample has 1 to 32 ids of each table. `table_order`: each table number once.
All inputs are finite; a program needn't handle non-finite values.
Results may differ from the reference program's by a relative error of at most 0.00007.
Values sent between devices are 32-bit elements; how exact they have to be, the bound alone decides.
A program may use at most 128 MiB of HBM per device.

```python
import math
import jax
import jax.numpy as jnp
import numpy as np
from jax import lax

D = 128
TABLES = 32
RS = 512
SAMP_DEV = 16
BAG_MOST = 32
IDS_DEV = 128
RB = 1024
CAP = 24
SAMPLES = 512
N_ROW = 16
DEVICES = 32


def touch_ends(entries, stream_key, smallest, largest):
    extent = entries.shape
    spot = [jax.random.randint(jax.random.fold_in(stream_key, axis), (), 0, extent[axis]) for axis in range(len(extent))]
    entries = entries.at[tuple(spot)].set(smallest)
    longest = extent.index(max(extent))
    spot[longest] = (spot[longest] + 1) % extent[longest]
    return entries.at[tuple(spot)].set(largest)


def shard_levels(rng, extent, pieces, low, high):
    level = 1.0
    for axis_at, blocks in pieces:
        heights = jax.random.uniform(jax.random.fold_in(jax.random.fold_in(rng, 6), axis_at), (blocks,), jnp.float32, low / len(pieces), high / len(pieces))
        level = level * jnp.repeat(jnp.exp(heights), extent[axis_at] // blocks).reshape((-1,) + (1,) * (len(extent) - 1 - axis_at))
    return level


def rank_table(count, skew):
    loads = [(1 << 20) // math.isqrt(standing ** skew) + 1 for standing in range(1, count + 1)]
    scale = 1 + sum(loads) // (1 << 30)
    return np.cumsum(np.array([max(1, weight // scale) for weight in loads]))


def ranked(rng, extent, number_of, slope):
    table = rank_table(number_of, slope)
    pick = jax.random.randint(jax.random.fold_in(rng, 1), extent, 0, int(table[number_of - 1]))
    standing = jnp.searchsorted(jnp.asarray(table, jnp.int32), pick, side="right")
    return jax.random.permutation(jax.random.fold_in(rng, 2), number_of)[standing].astype(jnp.int32)


def split_up(number_of, total, bound, lean):
    portions = [(1 << 20) // math.isqrt(standing ** lean) + 1 for standing in range(2, number_of + 1)]
    surplus, counts = total - bound - (number_of - 1), [1] * (number_of - 1)
    while surplus > 0:
        free = [i for i in range(number_of - 1) if counts[i] < bound]
        whole, remaining = sum([portions[i] for i in free]), surplus
        for i in free:
            extra = min(bound - counts[i], max(1, remaining * portions[i] // whole), surplus)
            counts[i] = counts[i] + extra
            surplus = surplus - extra
    return np.array([bound] + counts)


def ragged(own_key, amount, total, most, slope):
    if amount == 2:
        one = jax.random.randint(own_key, (), max(1, total - most), min(most, total - 1) + 1)
        return jnp.stack([one, total - one])
    tallies = jnp.asarray(split_up(amount, total, most, slope), jnp.int32)
    couples = (amount - 1) // 2
    donor, receiver = tallies[1:1 + 2 * couples:2], tallies[2:2 + 2 * couples:2]
    margin = jnp.minimum(donor - 1, most - receiver)
    moved = jax.random.randint(jax.random.fold_in(own_key, 1), (couples,), 0, 1 << 20) % (margin + 1)
    tallies = tallies.at[1:1 + 2 * couples:2].set(donor - moved).at[2:2 + 2 * couples:2].set(receiver + moved)
    return tallies[jax.random.permutation(jax.random.fold_in(own_key, 2), amount)]


def assign_block(key, own, number, rows, number_of, top, limit, slope):
    sequence = jax.random.permutation(key, number_of)
    packed, ordinary = load_shares(number_of, rows * top, limit, slope, True), load_shares(number_of, rows * top, limit, slope, False)
    places = jnp.arange(number_of)

    def named(sizes, turn):
        used = int((sizes > 0).sum())
        fixed = max(1, used // 4)
        passed = fixed + (places - fixed + turn * (used - fixed)) % max(1, number_of - fixed)
        return jnp.zeros((number_of,), jnp.int32).at[sequence[jnp.where(places < fixed, places, passed)]].set(jnp.asarray(sizes, jnp.int32))

    sizes = jnp.where(number % 4 == 0, named(packed, number // 4), named(ordinary, number - number // 4 - 1))
    mixed = jax.random.permutation(jax.random.fold_in(own, 3), number_of)
    giver, sink = mixed[0:number_of // 2 * 2:2], mixed[1:number_of // 2 * 2:2]
    margin = jnp.minimum(sizes[giver] - 1, limit - sizes[sink]) // 2
    margin = jnp.where((giver == sequence[0]) | (sink == sequence[0]) | (sizes[sink] == 0), 0, jnp.maximum(margin, 0))
    passed = jax.random.randint(jax.random.fold_in(own, 4), (number_of // 2,), 0, 1 << 20) % (margin + 1)
    sizes = sizes.at[giver].add(-passed).at[sink].add(passed)
    members = jnp.searchsorted(jnp.cumsum(sizes), jnp.arange(rows * top), side="right").astype(jnp.int32)
    table = members.reshape(top, rows).T
    table = table[jax.random.permutation(jax.random.fold_in(own, 1), rows)]
    turn = jax.random.randint(jax.random.fold_in(own, 2), (rows, 1), 0, top)
    return jnp.take_along_axis(table, (jnp.arange(top)[None, :] + turn) % top, axis=1)


def load_shares(number_of, total, most, skew, full):
    weights = [(1 << 20) // math.isqrt(standing ** skew) + 1 for standing in range(1, number_of + 1)]
    largest = most if full else min(most, max(-(-total // number_of), total * weights[0] // sum(weights)))
    least = 1 if total - largest >= number_of - 1 else 0
    given, surplus = [largest] + [least] * (number_of - 1), total - largest - least * (number_of - 1)
    while surplus > 0:
        movable = [i for i in range(1, number_of) if given[i] < largest] or [i for i in range(1, number_of) if given[i] < most]
        pool, left = sum([weights[i] for i in movable]), surplus
        for i in movable:
            addition = min(most - given[i], max(1, left * weights[i] // pool), surplus)
            given[i] = given[i] + addition
            surplus = surplus - addition
    return np.array(given)


def normal_values(own_key, shape, spread, bound, shards=(), kind=jnp.bfloat16):
    drawn = spread * jax.random.normal(own_key, shape, jnp.float32)
    if shards:
        drawn = drawn * shard_levels(own_key, shape, shards, -0.22, 0.18)
    return jnp.clip(drawn, -bound, bound).astype(kind)


def setup_inputs(seed: int = 0) -> dict:
    arg_keys = jax.random.split(jax.random.key(seed), 6)
    saved_rows = normal_values(arg_keys[0], (TABLES, RS, DEVICES, D), 0.5, 3.0, ((2, 32),), jnp.float32)
    table_order = jax.random.permutation(arg_keys[1], TABLES).astype(jnp.int32)
    owner_shard_keys = jax.random.split(jax.random.fold_in(arg_keys[2], 1), TABLES * DEVICES * IDS_DEV // IDS_DEV)
    owner_shard_turns = jax.random.permutation(jax.random.fold_in(arg_keys[2], 3), TABLES * DEVICES * IDS_DEV // IDS_DEV)
    owner_shard = jax.vmap(lambda own, number: assign_block(jax.random.fold_in(arg_keys[2], 2), own, number, IDS_DEV, N_ROW, 1, CAP, 2))(owner_shard_keys, owner_shard_turns).reshape((TABLES, DEVICES, IDS_DEV, 1))
    row_in_shard = touch_ends(ranked(arg_keys[3], (TABLES, DEVICES, IDS_DEV), RB, 2), jax.random.fold_in(arg_keys[3], 3), 0, RB - 1).astype(jnp.int32)
    bag_owner = jax.vmap(lambda own: jnp.searchsorted(jnp.cumsum(ragged(own, SAMP_DEV, IDS_DEV, BAG_MOST, 2)), jnp.arange(IDS_DEV), side="right"))(jax.random.split(arg_keys[4], TABLES * DEVICES)).reshape((TABLES, DEVICES, IDS_DEV)).astype(jnp.int32)
    return dict(saved_rows=saved_rows, table_order=table_order, owner_shard=owner_shard, row_in_shard=row_in_shard, bag_owner=bag_owner)


def pool_table(operands):
    one_table, shard_ids, local_ids, bag_ids = operands
    fetched = one_table[shard_ids * RB + local_ids]
    sample_ids = bag_ids + SAMP_DEV * jnp.arange(DEVICES, dtype=jnp.int32)[:, None]
    return jax.ops.segment_sum(fetched.reshape(-1, D), sample_ids.reshape(-1), num_segments=SAMPLES)


def reference(saved_rows, table_order, owner_shard, row_in_shard, bag_owner):
    tables = saved_rows.reshape(TABLES, RS * DEVICES, D)[table_order]
    per_table = lax.map(pool_table, (tables, owner_shard[table_order][..., 0], row_in_shard[table_order], bag_owner[table_order]))
    return jnp.transpose(per_table, (1, 0, 2))
```

```python
import functools

import jax
import jax.numpy as jnp
from jax import lax
from jax.experimental import pallas as pl
from jax.experimental.pallas import tpu as pltpu
from jax.sharding import PartitionSpec as P

SAMP_DEV = 16
MESH = pl.DeviceIdType.MESH
BF16 = jnp.bfloat16


def pool_kernel(groups, shards, order_ref, ids_ref, saved_ref, out_ref,
                rows, split, counts, part, got1, got2, got3, mine, res,
                row_sem, swap_send, swap_recv, send1, recv1, send2, recv2, send3, recv3, last_send, last_recv):
    half, _, depth, columns = rows.shape
    tables = 2 * half
    far = shards // 4
    devices = groups * shards
    assert devices & (devices - 1) == 0
    q_high = depth // 128
    samples = SAMP_DEV
    pair = 2 * samples
    g = lax.axis_index("grp")
    row = lax.axis_index("row")
    core = lax.rem(row, 2)
    m = lax.rem(row // 2, 2)
    a = row // 4
    chip = (g * shards + row) // 2
    flip = 1 - 2 * core

    def place(gg, aa, mm, cc):
        return (gg, (aa * 2 + mm) * 2 + cc)

    sibling = place(g, a, m, 1 - core)
    is0 = 1 - core
    near1 = place(lax.rem(g + is0, 2), a, lax.rem(m + core, 2), core)
    near2 = place(lax.rem(g + core, 2), a, lax.rem(m + is0, 2), core)

    def far_place(d):
        return place(g, lax.rem(a + d, far), m, core)

    barrier = pltpu.get_barrier_semaphore()
    for peer in [sibling, near1, near2] + [far_place(d) for d in range(1, far)]:
        pl.semaphore_signal(barrier, inc=1, device_id=peer, device_id_type=MESH)
    pl.semaphore_wait(barrier, 2 + far)

    def own_rows(t):
        return pltpu.make_async_copy(saved_ref.at[core * half + t], rows.at[t, core], row_sem.at[t])

    def swap_rows(t):
        return pltpu.make_async_remote_copy(
            src_ref=saved_ref.at[(1 - core) * half + t], dst_ref=rows.at[t, core],
            send_sem=swap_send.at[t], recv_sem=swap_recv.at[t], device_id=sibling, device_id_type=MESH)

    def swap_got(t):
        return pltpu.make_async_remote_copy(
            src_ref=saved_ref.at[(1 - core) * half + t], dst_ref=rows.at[t, 1 - core],
            send_sem=swap_send.at[t], recv_sem=swap_recv.at[t], device_id=sibling, device_id_type=MESH)

    def first(t):
        return pltpu.make_async_remote_copy(
            src_ref=part.at[t, 1], dst_ref=got1.at[t], send_sem=send1.at[t], recv_sem=recv1.at[t],
            device_id=near1, device_id_type=MESH)

    def second(t):
        return pltpu.make_async_remote_copy(
            src_ref=part.at[t, 0, 1], dst_ref=got2.at[t], send_sem=send2.at[t], recv_sem=recv2.at[t],
            device_id=near2, device_id_type=MESH)

    def third(t, d):
        return pltpu.make_async_remote_copy(
            src_ref=part.at[t, 0, 0, lax.rem(a + d, far)], dst_ref=got3.at[t, d - 1],
            send_sem=send3.at[t, d - 1], recv_sem=recv3.at[t, d - 1],
            device_id=far_place(d), device_id_type=MESH)

    def start_rows(t, carry):
        own_rows(t).start()
        swap_rows(t).start()
        return carry

    lax.fori_loop(0, half, start_rows, 0)

    key_rows = 2 * q_high * samples
    key_iota = lax.broadcasted_iota(jnp.int32, (key_rows, 128), 0)
    low_iota = lax.broadcasted_iota(jnp.int32, (128, 128), 0)

    def split_rows(t):
        own_rows(t).wait()
        swap_got(t).wait_recv()
        for k in range(2):
            x = rows[t, k]
            high = x.astype(BF16)
            split[k * depth:(k + 1) * depth, 0:columns] = high
            split[k * depth:(k + 1) * depth, columns:] = (x - high.astype(jnp.float32)).astype(BF16)

    def product(t, side):
        u = core * half + t
        per_side = 2 * far * 2

        def one(r, carry):
            c2 = lax.rem(r, 2)
            aa = lax.rem(r // 2, far)
            p2 = r // (2 * far)
            gg = lax.rem(g + is0 * side + core * p2, 2)
            mm = lax.rem(m + core * side + is0 * p2, 2)
            j = gg * shards + (aa * 2 + mm) * 2 + c2
            ids = ids_ref[j, pl.ds(u, 1), :]
            bag = ids_ref[j, pl.ds(tables + u, 1), :]
            dev = ids & (devices - 1)
            q = ids >> (devices.bit_length() - 1)
            key = ((dev & 1) * q_high + (q >> 7)) * samples + bag
            key = jnp.where((dev >> 1) == chip, key, -1)
            low = q & 127
            lhs = jnp.where(key == key_iota, 1.0, 0.0).astype(BF16)
            rhs = jnp.where(low == low_iota, 1.0, 0.0).astype(BF16)
            c = lax.dot_general(lhs, rhs, (((1,), (1,)), ((), ())), preferred_element_type=jnp.float32).astype(BF16)
            at = pl.ds(pl.multiple_of(r * samples, samples), samples)
            for i in range(2 * q_high):
                counts[at, i * 128:(i + 1) * 128] = c[i * samples:(i + 1) * samples]
            return carry

        lax.fori_loop(0, per_side, one, 0, unroll=4)
        for p2 in range(2):
            for_rows = counts[p2 * far * pair:(p2 + 1) * far * pair, :]
            both = jnp.dot(for_rows, split[...], preferred_element_type=jnp.float32)
            part[t, side, p2] = (both[:, :columns] + both[:, columns:]).reshape(far, pair, columns)

    def step(i, carry):
        @pl.when(i < half)
        def _():
            split_rows(i)
            product(i, 1)
            first(i).start()

        @pl.when(jnp.logical_and(i >= 1, i < half + 1))
        def _():
            t = i - 1
            first(t).wait_recv()
            part[t, 0, 1] += got1[t, 1]
            second(t).start()
            part[t, 0, 0] += got1[t, 0]

        @pl.when(jnp.logical_and(i >= 2, i < half + 2))
        def _():
            t = i - 2
            second(t).wait_recv()
            part[t, 0, 0] += got2[t]
            for d in range(1, far):
                third(t, d).start()

        @pl.when(jnp.logical_and(i >= 3, i < half + 3))
        def _():
            t = i - 3
            total = part[t, 0, 0, a]
            for d in range(1, far):
                third(t, d).wait_recv()
                total = total + got3[t, d - 1]
            mine[t] = total

        @pl.when(i < half)
        def _():
            product(i, 0)

        return carry

    lax.fori_loop(0, half + 3, step, 0)

    def hand_over(t, carry):
        res[core * half + t] = mine[t, pl.ds(pl.multiple_of(core * samples, samples), samples), :]
        return carry

    last = pltpu.make_async_remote_copy(
        src_ref=mine.at[:, pl.ds(pl.multiple_of((1 - core) * samples, samples), samples), :],
        dst_ref=res.at[pl.ds(core * half, half)],
        send_sem=last_send, recv_sem=last_recv, device_id=sibling, device_id_type=MESH)
    last.start()
    lax.fori_loop(0, half, hand_over, 0)

    def drain(t, carry):
        swap_rows(t).wait_send()
        first(t).wait_send()
        second(t).wait_send()
        for d in range(1, far):
            third(t, d).wait_send()
        return carry

    lax.fori_loop(0, half, drain, 0)
    last.wait()
    for c in range(tables):
        out_ref[:, c, :] = res[order_ref[c]]


def body(saved_rows, table_order, owner_shard, row_in_shard, bag_owner):
    groups = lax.axis_size("grp")
    shards = lax.axis_size("row")
    devices = groups * shards
    tables, depth, _, columns = saved_rows.shape
    half = tables // 2
    far = shards // 4
    shard_rows = depth * devices // shards
    ids = owner_shard[:, 0, :, 0] * shard_rows + row_in_shard[:, 0, :]
    wanted = lax.all_gather(jnp.concatenate([ids, bag_owner[:, 0, :]], axis=0), ("grp", "row"))
    pair = 2 * SAMP_DEV
    f32 = jnp.float32
    dma = pltpu.SemaphoreType.DMA
    return pl.pallas_call(
        functools.partial(pool_kernel, groups, shards),
        out_shape=jax.ShapeDtypeStruct((SAMP_DEV, tables, columns), f32),
        in_specs=[
            pl.BlockSpec(memory_space=pltpu.SMEM),
            pl.BlockSpec(memory_space=pltpu.VMEM),
            pl.BlockSpec(memory_space=pl.ANY),
        ],
        out_specs=pl.BlockSpec(memory_space=pltpu.VMEM),
        scratch_shapes=[
            pltpu.VMEM((half, 2, depth, columns), f32),
            pltpu.VMEM((2 * depth, 2 * columns), BF16),
            pltpu.VMEM((2 * far * pair, 2 * depth), BF16),
            pltpu.VMEM((half, 2, 2, far, pair, columns), f32),
            pltpu.VMEM((half, 2, far, pair, columns), f32),
            pltpu.VMEM((half, far, pair, columns), f32),
            pltpu.VMEM((half, far - 1, pair, columns), f32),
            pltpu.VMEM((half, pair, columns), f32),
            pltpu.VMEM((tables, SAMP_DEV, columns), f32),
            dma((half,)), dma((half,)), dma((half,)),
            dma((half,)), dma((half,)), dma((half,)), dma((half,)),
            dma((half, far - 1)), dma((half, far - 1)),
            dma, dma,
        ],
        compiler_params=pltpu.CompilerParams(collective_id=0, has_side_effects=True),
    )(table_order, wanted, saved_rows.reshape(tables, depth, columns))


def solution(mesh):
    return jax.shard_map(
        body,
        mesh=mesh,
        in_specs=(
            P(None, None, ("grp", "row"), None),
            P(),
            P(None, ("grp", "row"), None, None),
            P(None, ("grp", "row"), None),
            P(None, ("grp", "row"), None),
        ),
        out_specs=P(("grp", "row"), None, None),
        check_vma=False,
    )
```

```python
import functools

import jax
import jax.numpy as jnp
from jax import lax
from jax.experimental import pallas as pl
from jax.experimental.pallas import tpu as pltpu
from jax.sharding import PartitionSpec as P

SAMP_DEV = 16
MESH = pl.DeviceIdType.MESH
BF16 = jnp.bfloat16


def pool_kernel(groups, shards, order_ref, own_ref, saved_ref, out_ref,
                ids, own_sem, ask0_send, ask0_recv, ask3_send, ask3_recv, ask2_send, ask2_recv,
                ask1_send, ask1_recv, ask12_send, ask12_recv,
                rows, split, counts, part, got1, got2, got3, mine, res,
                row_sem, swap_send, swap_recv, send1, recv1, send2, recv2, send3, recv3, last_send, last_recv):
    half, _, depth, columns = rows.shape
    tables = 2 * half
    far = shards // 4
    devices = groups * shards
    assert devices & (devices - 1) == 0
    q_high = depth // 128
    samples = SAMP_DEV
    pair = 2 * samples
    g = lax.axis_index("grp")
    row = lax.axis_index("row")
    core = lax.rem(row, 2)
    m = lax.rem(row // 2, 2)
    a = row // 4
    chip = (g * shards + row) // 2
    flip = 1 - 2 * core

    def place(gg, aa, mm, cc):
        return (gg, (aa * 2 + mm) * 2 + cc)

    sibling = place(g, a, m, 1 - core)
    is0 = 1 - core
    near1 = place(lax.rem(g + is0, 2), a, lax.rem(m + core, 2), core)
    near2 = place(lax.rem(g + core, 2), a, lax.rem(m + is0, 2), core)

    def far_place(d):
        return place(g, lax.rem(a + d, far), m, core)

    barrier = pltpu.get_barrier_semaphore()
    for peer in [sibling, near1, near2] + [far_place(d) for d in range(1, far)]:
        pl.semaphore_signal(barrier, inc=1, device_id=peer, device_id_type=MESH)
    pl.semaphore_wait(barrier, 2 + far)

    def own_rows(t):
        return pltpu.make_async_copy(saved_ref.at[core * half + t], rows.at[t, core], row_sem.at[t])

    def swap_rows(t):
        return pltpu.make_async_remote_copy(
            src_ref=saved_ref.at[(1 - core) * half + t], dst_ref=rows.at[t, core],
            send_sem=swap_send.at[t], recv_sem=swap_recv.at[t], device_id=sibling, device_id_type=MESH)

    def swap_got(t):
        return pltpu.make_async_remote_copy(
            src_ref=saved_ref.at[(1 - core) * half + t], dst_ref=rows.at[t, 1 - core],
            send_sem=swap_send.at[t], recv_sem=swap_recv.at[t], device_id=sibling, device_id_type=MESH)

    def first(t):
        return pltpu.make_async_remote_copy(
            src_ref=part.at[t, 1], dst_ref=got1.at[t], send_sem=send1.at[t], recv_sem=recv1.at[t],
            device_id=near1, device_id_type=MESH)

    def second(t):
        return pltpu.make_async_remote_copy(
            src_ref=part.at[t, 0, 1], dst_ref=got2.at[t], send_sem=send2.at[t], recv_sem=recv2.at[t],
            device_id=near2, device_id_type=MESH)

    def third(t, d):
        return pltpu.make_async_remote_copy(
            src_ref=part.at[t, 0, 0, lax.rem(a + d, far)], dst_ref=got3.at[t, d - 1],
            send_sem=send3.at[t, d - 1], recv_sem=recv3.at[t, d - 1],
            device_id=far_place(d), device_id_type=MESH)

    def start_rows(t, carry):
        own_rows(t).start()
        swap_rows(t).start()
        return carry

    def keep_ids(k):
        return pltpu.make_async_copy(own_ref.at[core, k], ids.at[k, 0, 0, a, core], own_sem.at[k])

    def ask(src, dst, sends, recvs, peer):
        return pltpu.make_async_remote_copy(
            src_ref=src, dst_ref=dst, send_sem=sends, recv_sem=recvs, device_id=peer, device_id_type=MESH)

    def ask0(k):
        return ask(own_ref.at[1 - core, k], ids.at[k, 0, 0, a, core], ask0_send.at[k], ask0_recv.at[k], sibling)

    def ask3(k, d):
        return ask(ids.at[k, 0, 0, a], ids.at[k, 0, 0, a],
                   ask3_send.at[k, d - 1], ask3_recv.at[k, d - 1], far_place(d))

    def ask2(k):
        return ask(ids.at[k, 0, 0], ids.at[k, 0, 1], ask2_send.at[k], ask2_recv.at[k], near2)

    def ask1(k):
        return ask(ids.at[k, 0, 0], ids.at[k, 1, 0], ask1_send.at[k], ask1_recv.at[k], near1)

    def ask12(k):
        return ask(ids.at[k, 0, 1], ids.at[k, 1, 1], ask12_send.at[k], ask12_recv.at[k], near1)

    chunks = ids.shape[0]
    per_chunk = half // chunks
    for k in range(chunks):
        ask0(k).start()
        keep_ids(k).start()
    lax.fori_loop(0, half, start_rows, 0)
    for k in range(chunks):
        keep_ids(k).wait()
        ask0(k).wait_recv()
        for d in range(1, far):
            ask3(k, d).start()
    for k in range(chunks):
        for d in range(1, far):
            ask3(k, d).wait_recv()
        ask2(k).start()
        ask1(k).start()
    for k in range(chunks):
        ask2(k).wait_recv()
        ask12(k).start()

    key_rows = 2 * q_high * samples
    key_iota = lax.broadcasted_iota(jnp.int32, (key_rows, 128), 0)
    low_iota = lax.broadcasted_iota(jnp.int32, (128, 128), 0)

    def split_rows(t):
        own_rows(t).wait()
        swap_got(t).wait_recv()
        for k in range(2):
            x = rows[t, k]
            high = x.astype(BF16)
            split[k * depth:(k + 1) * depth, 0:columns] = high
            split[k * depth:(k + 1) * depth, columns:] = (x - high.astype(jnp.float32)).astype(BF16)

    def product(t, side):
        per_side = 2 * far * 2
        chunk = t // per_chunk
        slot = lax.rem(t, per_chunk)

        def one(r, carry):
            c2 = lax.rem(r, 2)
            aa = lax.rem(r // 2, far)
            p2 = r // (2 * far)
            block = ids.at[chunk, side, p2, aa, c2]
            want = block[pl.ds(slot, 1), :]
            bag = block[pl.ds(per_chunk + slot, 1), :]
            dev = want & (devices - 1)
            q = want >> (devices.bit_length() - 1)
            key = ((dev & 1) * q_high + (q >> 7)) * samples + bag
            key = jnp.where((dev >> 1) == chip, key, -1)
            low = q & 127
            lhs = jnp.where(key == key_iota, 1.0, 0.0).astype(BF16)
            rhs = jnp.where(low == low_iota, 1.0, 0.0).astype(BF16)
            c = lax.dot_general(lhs, rhs, (((1,), (1,)), ((), ())), preferred_element_type=jnp.float32).astype(BF16)
            at = pl.ds(pl.multiple_of(r * samples, samples), samples)
            for i in range(2 * q_high):
                counts[at, i * 128:(i + 1) * 128] = c[i * samples:(i + 1) * samples]
            return carry

        lax.fori_loop(0, per_side, one, 0, unroll=4)
        for p2 in range(2):
            for_rows = counts[p2 * far * pair:(p2 + 1) * far * pair, :]
            both = jnp.dot(for_rows, split[...], preferred_element_type=jnp.float32)
            part[t, side, p2] = (both[:, :columns] + both[:, columns:]).reshape(far, pair, columns)

    def step(i, carry):
        @pl.when(i < half)
        def _():
            @pl.when(lax.rem(i, per_chunk) == 0)
            def _():
                ask1(i // per_chunk).wait_recv()
                ask12(i // per_chunk).wait_recv()

            split_rows(i)
            product(i, 1)
            first(i).start()

        @pl.when(jnp.logical_and(i >= 1, i < half + 1))
        def _():
            t = i - 1
            first(t).wait_recv()
            part[t, 0, 1] += got1[t, 1]
            second(t).start()
            part[t, 0, 0] += got1[t, 0]

        @pl.when(jnp.logical_and(i >= 2, i < half + 2))
        def _():
            t = i - 2
            second(t).wait_recv()
            part[t, 0, 0] += got2[t]
            for d in range(1, far):
                third(t, d).start()

        @pl.when(jnp.logical_and(i >= 3, i < half + 3))
        def _():
            t = i - 3
            total = part[t, 0, 0, a]
            for d in range(1, far):
                third(t, d).wait_recv()
                total = total + got3[t, d - 1]
            mine[t] = total

        @pl.when(i < half)
        def _():
            product(i, 0)

        return carry

    lax.fori_loop(0, half + 3, step, 0)

    def hand_over(t, carry):
        res[core * half + t] = mine[t, pl.ds(pl.multiple_of(core * samples, samples), samples), :]
        return carry

    last = pltpu.make_async_remote_copy(
        src_ref=mine.at[:, pl.ds(pl.multiple_of((1 - core) * samples, samples), samples), :],
        dst_ref=res.at[pl.ds(core * half, half)],
        send_sem=last_send, recv_sem=last_recv, device_id=sibling, device_id_type=MESH)
    last.start()
    lax.fori_loop(0, half, hand_over, 0)

    def drain(t, carry):
        swap_rows(t).wait_send()
        first(t).wait_send()
        second(t).wait_send()
        for d in range(1, far):
            third(t, d).wait_send()
        return carry

    lax.fori_loop(0, half, drain, 0)
    for k in range(chunks):
        ask0(k).wait_send()
        for d in range(1, far):
            ask3(k, d).wait_send()
        ask2(k).wait_send()
        ask1(k).wait_send()
        ask12(k).wait_send()
    last.wait()
    for c in range(tables):
        out_ref[:, c, :] = res[order_ref[c]]


def body(saved_rows, table_order, owner_shard, row_in_shard, bag_owner):
    groups = lax.axis_size("grp")
    shards = lax.axis_size("row")
    devices = groups * shards
    tables, depth, _, columns = saved_rows.shape
    half = tables // 2
    far = shards // 4
    shard_rows = depth * devices // shards
    ids = owner_shard[:, 0, :, 0] * shard_rows + row_in_shard[:, 0, :]
    chunks = max(1, half // 4)
    per_chunk = half // chunks
    cut = (2, chunks, per_chunk, ids.shape[-1])
    wanted = jnp.concatenate([ids.reshape(cut), bag_owner[:, 0, :].reshape(cut)], axis=2)
    pair = 2 * SAMP_DEV
    f32 = jnp.float32
    dma = pltpu.SemaphoreType.DMA
    return pl.pallas_call(
        functools.partial(pool_kernel, groups, shards),
        out_shape=jax.ShapeDtypeStruct((SAMP_DEV, tables, columns), f32),
        in_specs=[
            pl.BlockSpec(memory_space=pltpu.SMEM),
            pl.BlockSpec(memory_space=pltpu.VMEM),
            pl.BlockSpec(memory_space=pl.ANY),
        ],
        out_specs=pl.BlockSpec(memory_space=pltpu.VMEM),
        scratch_shapes=[
            pltpu.VMEM((chunks, 2, 2, far, 2, 2 * per_chunk, ids.shape[-1]), jnp.int32),
            dma((chunks,)), dma((chunks,)), dma((chunks,)),
            dma((chunks, far - 1)), dma((chunks, far - 1)),
            dma((chunks,)), dma((chunks,)), dma((chunks,)), dma((chunks,)), dma((chunks,)), dma((chunks,)),
            pltpu.VMEM((half, 2, depth, columns), f32),
            pltpu.VMEM((2 * depth, 2 * columns), BF16),
            pltpu.VMEM((2 * far * pair, 2 * depth), BF16),
            pltpu.VMEM((half, 2, 2, far, pair, columns), f32),
            pltpu.VMEM((half, 2, far, pair, columns), f32),
            pltpu.VMEM((half, far, pair, columns), f32),
            pltpu.VMEM((half, far - 1, pair, columns), f32),
            pltpu.VMEM((half, pair, columns), f32),
            pltpu.VMEM((tables, SAMP_DEV, columns), f32),
            dma((half,)), dma((half,)), dma((half,)),
            dma((half,)), dma((half,)), dma((half,)), dma((half,)),
            dma((half, far - 1)), dma((half, far - 1)),
            dma, dma,
        ],
        compiler_params=pltpu.CompilerParams(collective_id=0, has_side_effects=True),
    )(table_order, wanted, saved_rows.reshape(tables, depth, columns))


def solution(mesh):
    return jax.shard_map(
        body,
        mesh=mesh,
        in_specs=(
            P(None, None, ("grp", "row"), None),
            P(),
            P(None, ("grp", "row"), None, None),
            P(None, ("grp", "row"), None),
            P(None, ("grp", "row"), None),
        ),
        out_specs=P(("grp", "row"), None, None),
        check_vma=False,
    )
```

```python
import functools

import jax
import jax.numpy as jnp
from jax import lax
from jax.experimental import pallas as pl
from jax.experimental.pallas import tpu as pltpu
from jax.sharding import PartitionSpec as P

SAMP_DEV = 16
LAG = 2
MESH = pl.DeviceIdType.MESH
BF16 = jnp.bfloat16


def pool_kernel(groups, shards, order_ref, own_ref, saved_ref, out_ref,
                ids, own_sem, ask0_send, ask0_recv, ask3_send, ask3_recv, ask2_send, ask2_recv,
                ask1_send, ask1_recv, ask12_send, ask12_recv,
                rows, split, counts, part, got1, got2, got3, mine, res,
                row_sem, swap_send, swap_recv, send1, recv1, send2, recv2, send3, recv3, last_send, last_recv):
    half, _, depth, columns = rows.shape
    tables = 2 * half
    far = shards // 4
    devices = groups * shards
    assert devices & (devices - 1) == 0
    q_high = depth // 128
    samples = SAMP_DEV
    pair = 2 * samples
    g = lax.axis_index("grp")
    row = lax.axis_index("row")
    core = lax.rem(row, 2)
    m = lax.rem(row // 2, 2)
    a = row // 4
    chip = (g * shards + row) // 2
    flip = 1 - 2 * core

    def place(gg, aa, mm, cc):
        return (gg, (aa * 2 + mm) * 2 + cc)

    sibling = place(g, a, m, 1 - core)
    is0 = 1 - core
    near1 = place(lax.rem(g + is0, 2), a, lax.rem(m + core, 2), core)
    near2 = place(lax.rem(g + core, 2), a, lax.rem(m + is0, 2), core)

    def far_place(d):
        return place(g, lax.rem(a + d, far), m, core)

    barrier = pltpu.get_barrier_semaphore()
    for peer in [sibling, near1, near2] + [far_place(d) for d in range(1, far)]:
        pl.semaphore_signal(barrier, inc=1, device_id=peer, device_id_type=MESH)
    pl.semaphore_wait(barrier, 2 + far)

    def own_rows(t):
        return pltpu.make_async_copy(saved_ref.at[core * half + t], rows.at[t, core], row_sem.at[t])

    def swap_rows(t):
        return pltpu.make_async_remote_copy(
            src_ref=saved_ref.at[(1 - core) * half + t], dst_ref=rows.at[t, core],
            send_sem=swap_send.at[t], recv_sem=swap_recv.at[t], device_id=sibling, device_id_type=MESH)

    def swap_got(t):
        return pltpu.make_async_remote_copy(
            src_ref=saved_ref.at[(1 - core) * half + t], dst_ref=rows.at[t, 1 - core],
            send_sem=swap_send.at[t], recv_sem=swap_recv.at[t], device_id=sibling, device_id_type=MESH)

    def first(t):
        return pltpu.make_async_remote_copy(
            src_ref=part.at[t, 1], dst_ref=got1.at[t], send_sem=send1.at[t], recv_sem=recv1.at[t],
            device_id=near1, device_id_type=MESH)

    def second(t):
        return pltpu.make_async_remote_copy(
            src_ref=part.at[t, 0, 1], dst_ref=got2.at[t], send_sem=send2.at[t], recv_sem=recv2.at[t],
            device_id=near2, device_id_type=MESH)

    def third(t, d):
        return pltpu.make_async_remote_copy(
            src_ref=part.at[t, 0, 0, lax.rem(a + d, far)], dst_ref=got3.at[t, d - 1],
            send_sem=send3.at[t, d - 1], recv_sem=recv3.at[t, d - 1],
            device_id=far_place(d), device_id_type=MESH)

    def start_rows(t, carry):
        own_rows(t).start()
        swap_rows(t).start()
        return carry

    def keep_ids(k):
        return pltpu.make_async_copy(own_ref.at[core, k], ids.at[k, 0, 0, a, core], own_sem.at[k])

    def ask(src, dst, sends, recvs, peer):
        return pltpu.make_async_remote_copy(
            src_ref=src, dst_ref=dst, send_sem=sends, recv_sem=recvs, device_id=peer, device_id_type=MESH)

    def ask0(k):
        return ask(own_ref.at[1 - core, k], ids.at[k, 0, 0, a, core], ask0_send.at[k], ask0_recv.at[k], sibling)

    def ask3(k, d):
        return ask(ids.at[k, 0, 0, a], ids.at[k, 0, 0, a],
                   ask3_send.at[k, d - 1], ask3_recv.at[k, d - 1], far_place(d))

    def ask2(k):
        return ask(ids.at[k, 0, 0], ids.at[k, 0, 1], ask2_send.at[k], ask2_recv.at[k], near2)

    def ask1(k):
        return ask(ids.at[k, 0, 0], ids.at[k, 1, 0], ask1_send.at[k], ask1_recv.at[k], near1)

    def ask12(k):
        return ask(ids.at[k, 0, 1], ids.at[k, 1, 1], ask12_send.at[k], ask12_recv.at[k], near1)

    chunks = ids.shape[0]
    per_chunk = half // chunks
    for k in range(chunks):
        ask0(k).start()
        keep_ids(k).start()
    lax.fori_loop(0, half, start_rows, 0)
    for k in range(chunks):
        keep_ids(k).wait()
        ask0(k).wait_recv()
        for d in range(1, far):
            ask3(k, d).start()

    def ask_near(k):
        for d in range(1, far):
            ask3(k, d).wait_recv()
        ask2(k).start()
        ask1(k).start()

    def ask_last(k):
        ask2(k).wait_recv()
        ask12(k).start()

    ask_near(0)
    ask_last(0)

    key_rows = 2 * q_high * samples
    key_iota = lax.broadcasted_iota(jnp.int32, (key_rows, 128), 0)
    low_iota = lax.broadcasted_iota(jnp.int32, (128, 128), 0)

    def split_rows(t):
        own_rows(t).wait()
        swap_got(t).wait_recv()
        for k in range(2):
            x = rows[t, k]
            high = x.astype(BF16)
            split[k * depth:(k + 1) * depth, 0:columns] = high
            split[k * depth:(k + 1) * depth, columns:] = (x - high.astype(jnp.float32)).astype(BF16)

    def product(t, side):
        per_side = 2 * far * 2
        chunk = t // per_chunk
        slot = lax.rem(t, per_chunk)

        def one(r, carry):
            c2 = lax.rem(r, 2)
            aa = lax.rem(r // 2, far)
            p2 = r // (2 * far)
            block = ids.at[chunk, side, p2, aa, c2]
            want = block[pl.ds(slot, 1), :]
            bag = block[pl.ds(per_chunk + slot, 1), :]
            dev = want & (devices - 1)
            q = want >> (devices.bit_length() - 1)
            key = ((dev & 1) * q_high + (q >> 7)) * samples + bag
            key = jnp.where((dev >> 1) == chip, key, -1)
            low = q & 127
            lhs = jnp.where(key == key_iota, 1.0, 0.0).astype(BF16)
            rhs = jnp.where(low == low_iota, 1.0, 0.0).astype(BF16)
            c = lax.dot_general(lhs, rhs, (((1,), (1,)), ((), ())), preferred_element_type=jnp.float32).astype(BF16)
            at = pl.ds(pl.multiple_of(r * samples, samples), samples)
            for i in range(2 * q_high):
                counts[at, i * 128:(i + 1) * 128] = c[i * samples:(i + 1) * samples]
            return carry

        lax.fori_loop(0, per_side, one, 0, unroll=4)
        for p2 in range(2):
            for_rows = counts[p2 * far * pair:(p2 + 1) * far * pair, :]
            both = jnp.dot(for_rows, split[...], preferred_element_type=jnp.float32)
            part[t, side, p2] = (both[:, :columns] + both[:, columns:]).reshape(far, pair, columns)

    def step(i, carry):
        ahead = i // per_chunk + 1
        for turn, stage in enumerate((ask_near, ask_last)):
            @pl.when(jnp.logical_and(lax.rem(i, per_chunk) == turn, ahead < chunks))
            def _(stage=stage):
                stage(ahead)

        @pl.when(i < half)
        def _():
            @pl.when(lax.rem(i, per_chunk) == 0)
            def _():
                ask1(i // per_chunk).wait_recv()
                ask12(i // per_chunk).wait_recv()

            split_rows(i)
            product(i, 1)
            first(i).start()

        @pl.when(jnp.logical_and(i >= LAG, i < half + LAG))
        def _():
            t = i - LAG
            first(t).wait_recv()
            part[t, 0, 1] += got1[t, 1]
            second(t).start()
            part[t, 0, 0] += got1[t, 0]

        @pl.when(jnp.logical_and(i >= 2 * LAG, i < half + 2 * LAG))
        def _():
            t = i - 2 * LAG
            second(t).wait_recv()
            part[t, 0, 0] += got2[t]
            for d in range(1, far):
                third(t, d).start()

        @pl.when(jnp.logical_and(i >= 3 * LAG, i < half + 3 * LAG))
        def _():
            t = i - 3 * LAG
            total = part[t, 0, 0, a]
            for d in range(1, far):
                third(t, d).wait_recv()
                total = total + got3[t, d - 1]
            mine[t] = total

        @pl.when(i < half)
        def _():
            product(i, 0)

        return carry

    lax.fori_loop(0, half + 3 * LAG, step, 0)

    def hand_over(t, carry):
        res[core * half + t] = mine[t, pl.ds(pl.multiple_of(core * samples, samples), samples), :]
        return carry

    last = pltpu.make_async_remote_copy(
        src_ref=mine.at[:, pl.ds(pl.multiple_of((1 - core) * samples, samples), samples), :],
        dst_ref=res.at[pl.ds(core * half, half)],
        send_sem=last_send, recv_sem=last_recv, device_id=sibling, device_id_type=MESH)
    last.start()
    lax.fori_loop(0, half, hand_over, 0)

    def drain(t, carry):
        swap_rows(t).wait_send()
        first(t).wait_send()
        second(t).wait_send()
        for d in range(1, far):
            third(t, d).wait_send()
        return carry

    lax.fori_loop(0, half, drain, 0)
    for k in range(chunks):
        ask0(k).wait_send()
        for d in range(1, far):
            ask3(k, d).wait_send()
        ask2(k).wait_send()
        ask1(k).wait_send()
        ask12(k).wait_send()
    last.wait()
    for c in range(tables):
        out_ref[:, c, :] = res[order_ref[c]]


def body(saved_rows, table_order, owner_shard, row_in_shard, bag_owner):
    groups = lax.axis_size("grp")
    shards = lax.axis_size("row")
    devices = groups * shards
    tables, depth, _, columns = saved_rows.shape
    half = tables // 2
    far = shards // 4
    shard_rows = depth * devices // shards
    ids = owner_shard[:, 0, :, 0] * shard_rows + row_in_shard[:, 0, :]
    chunks = max(1, half // 4)
    per_chunk = half // chunks
    cut = (2, chunks, per_chunk, ids.shape[-1])
    wanted = jnp.concatenate([ids.reshape(cut), bag_owner[:, 0, :].reshape(cut)], axis=2)
    pair = 2 * SAMP_DEV
    f32 = jnp.float32
    dma = pltpu.SemaphoreType.DMA
    return pl.pallas_call(
        functools.partial(pool_kernel, groups, shards),
        out_shape=jax.ShapeDtypeStruct((SAMP_DEV, tables, columns), f32),
        in_specs=[
            pl.BlockSpec(memory_space=pltpu.SMEM),
            pl.BlockSpec(memory_space=pltpu.VMEM),
            pl.BlockSpec(memory_space=pl.ANY),
        ],
        out_specs=pl.BlockSpec(memory_space=pltpu.VMEM),
        scratch_shapes=[
            pltpu.VMEM((chunks, 2, 2, far, 2, 2 * per_chunk, ids.shape[-1]), jnp.int32),
            dma((chunks,)), dma((chunks,)), dma((chunks,)),
            dma((chunks, far - 1)), dma((chunks, far - 1)),
            dma((chunks,)), dma((chunks,)), dma((chunks,)), dma((chunks,)), dma((chunks,)), dma((chunks,)),
            pltpu.VMEM((half, 2, depth, columns), f32),
            pltpu.VMEM((2 * depth, 2 * columns), BF16),
            pltpu.VMEM((2 * far * pair, 2 * depth), BF16),
            pltpu.VMEM((half, 2, 2, far, pair, columns), f32),
            pltpu.VMEM((half, 2, far, pair, columns), f32),
            pltpu.VMEM((half, far, pair, columns), f32),
            pltpu.VMEM((half, far - 1, pair, columns), f32),
            pltpu.VMEM((half, pair, columns), f32),
            pltpu.VMEM((tables, SAMP_DEV, columns), f32),
            dma((half,)), dma((half,)), dma((half,)),
            dma((half,)), dma((half,)), dma((half,)), dma((half,)),
            dma((half, far - 1)), dma((half, far - 1)),
            dma, dma,
        ],
        compiler_params=pltpu.CompilerParams(collective_id=0, has_side_effects=True),
    )(table_order, wanted, saved_rows.reshape(tables, depth, columns))


def solution(mesh):
    return jax.shard_map(
        body,
        mesh=mesh,
        in_specs=(
            P(None, None, ("grp", "row"), None),
            P(),
            P(None, ("grp", "row"), None, None),
            P(None, ("grp", "row"), None),
            P(None, ("grp", "row"), None),
        ),
        out_specs=P(("grp", "row"), None, None),
        check_vma=False,
    )
```

```python
import functools

import jax
import jax.numpy as jnp
from jax import lax
from jax.experimental import pallas as pl
from jax.experimental.pallas import tpu as pltpu
from jax.sharding import PartitionSpec as P

SAMP_DEV = 16
UNROLL = 16
LAG = 2
MESH = pl.DeviceIdType.MESH
BF16 = jnp.bfloat16


def pool_kernel(groups, shards, order_ref, own_ref, saved_ref, out_ref,
                ids, own_sem, ask0_send, ask0_recv, ask3_send, ask3_recv, ask2_send, ask2_recv,
                ask1_send, ask1_recv, ask12_send, ask12_recv,
                rows, split, counts, part, got1, got2, got3, mine, res,
                row_sem, swap_send, swap_recv, send1, recv1, send2, recv2, send3, recv3, last_send, last_recv):
    half, _, depth, columns = rows.shape
    tables = 2 * half
    far = shards // 4
    devices = groups * shards
    assert devices & (devices - 1) == 0
    q_high = depth // 128
    samples = SAMP_DEV
    pair = 2 * samples
    g = lax.axis_index("grp")
    row = lax.axis_index("row")
    core = lax.rem(row, 2)
    m = lax.rem(row // 2, 2)
    a = row // 4
    chip = (g * shards + row) // 2
    flip = 1 - 2 * core

    def place(gg, aa, mm, cc):
        return (gg, (aa * 2 + mm) * 2 + cc)

    sibling = place(g, a, m, 1 - core)
    is0 = 1 - core
    near1 = place(lax.rem(g + is0, 2), a, lax.rem(m + core, 2), core)
    near2 = place(lax.rem(g + core, 2), a, lax.rem(m + is0, 2), core)

    def far_place(d):
        return place(g, lax.rem(a + d, far), m, core)

    barrier = pltpu.get_barrier_semaphore()
    for peer in [sibling, near1, near2] + [far_place(d) for d in range(1, far)]:
        pl.semaphore_signal(barrier, inc=1, device_id=peer, device_id_type=MESH)
    pl.semaphore_wait(barrier, 2 + far)

    def own_rows(t):
        return pltpu.make_async_copy(saved_ref.at[core * half + t], rows.at[t, core], row_sem.at[t])

    def swap_rows(t):
        return pltpu.make_async_remote_copy(
            src_ref=saved_ref.at[(1 - core) * half + t], dst_ref=rows.at[t, core],
            send_sem=swap_send.at[t], recv_sem=swap_recv.at[t], device_id=sibling, device_id_type=MESH)

    def swap_got(t):
        return pltpu.make_async_remote_copy(
            src_ref=saved_ref.at[(1 - core) * half + t], dst_ref=rows.at[t, 1 - core],
            send_sem=swap_send.at[t], recv_sem=swap_recv.at[t], device_id=sibling, device_id_type=MESH)

    def first(t):
        return pltpu.make_async_remote_copy(
            src_ref=part.at[t, 1], dst_ref=got1.at[t], send_sem=send1.at[t], recv_sem=recv1.at[t],
            device_id=near1, device_id_type=MESH)

    def second(t):
        return pltpu.make_async_remote_copy(
            src_ref=part.at[t, 0, 1], dst_ref=got2.at[t], send_sem=send2.at[t], recv_sem=recv2.at[t],
            device_id=near2, device_id_type=MESH)

    def third(t, d):
        return pltpu.make_async_remote_copy(
            src_ref=part.at[t, 0, 0, lax.rem(a + d, far)], dst_ref=got3.at[t, d - 1],
            send_sem=send3.at[t, d - 1], recv_sem=recv3.at[t, d - 1],
            device_id=far_place(d), device_id_type=MESH)

    def start_rows(t, carry):
        own_rows(t).start()
        swap_rows(t).start()
        return carry

    def keep_ids(k):
        return pltpu.make_async_copy(own_ref.at[core, k], ids.at[k, 0, 0, a, core], own_sem.at[k])

    def ask(src, dst, sends, recvs, peer):
        return pltpu.make_async_remote_copy(
            src_ref=src, dst_ref=dst, send_sem=sends, recv_sem=recvs, device_id=peer, device_id_type=MESH)

    def ask0(k):
        return ask(own_ref.at[1 - core, k], ids.at[k, 0, 0, a, core], ask0_send.at[k], ask0_recv.at[k], sibling)

    def ask3(k, d):
        return ask(ids.at[k, 0, 0, a], ids.at[k, 0, 0, a],
                   ask3_send.at[k, d - 1], ask3_recv.at[k, d - 1], far_place(d))

    def ask2(k):
        return ask(ids.at[k, 0, 0], ids.at[k, 0, 1], ask2_send.at[k], ask2_recv.at[k], near2)

    def ask1(k):
        return ask(ids.at[k, 0, 0], ids.at[k, 1, 0], ask1_send.at[k], ask1_recv.at[k], near1)

    def ask12(k):
        return ask(ids.at[k, 0, 1], ids.at[k, 1, 1], ask12_send.at[k], ask12_recv.at[k], near1)

    chunks = ids.shape[0]
    per_chunk = half // chunks
    for k in range(chunks):
        ask0(k).start()
        keep_ids(k).start()
    lax.fori_loop(0, half, start_rows, 0)
    for k in range(chunks):
        keep_ids(k).wait()
        ask0(k).wait_recv()
        for d in range(1, far):
            ask3(k, d).start()

    def ask_near(k):
        for d in range(1, far):
            ask3(k, d).wait_recv()
        ask2(k).start()
        ask1(k).start()

    def ask_last(k):
        ask2(k).wait_recv()
        ask12(k).start()

    ask_near(0)
    ask_last(0)

    key_rows = 2 * q_high * samples
    key_iota = lax.broadcasted_iota(jnp.int32, (key_rows, 128), 0)
    low_iota = lax.broadcasted_iota(jnp.int32, (128, 128), 0)

    def split_rows(t):
        own_rows(t).wait()
        swap_got(t).wait_recv()
        for k in range(2):
            x = rows[t, k]
            high = x.astype(BF16)
            split[k * depth:(k + 1) * depth, 0:columns] = high
            split[k * depth:(k + 1) * depth, columns:] = (x - high.astype(jnp.float32)).astype(BF16)

    def product(t):
        every = 2 * 2 * far * 2
        chunk = t // per_chunk
        slot = lax.rem(t, per_chunk)

        def one(r, carry):
            c2 = lax.rem(r, 2)
            aa = lax.rem(r // 2, far)
            p2 = lax.rem(r // (2 * far), 2)
            block = ids.at[chunk, r // (4 * far), p2, aa, c2]
            want = block[pl.ds(slot, 1), :]
            bag = block[pl.ds(per_chunk + slot, 1), :]
            dev = want & (devices - 1)
            q = want >> (devices.bit_length() - 1)
            key = ((dev & 1) * q_high + (q >> 7)) * samples + bag
            key = jnp.where((dev >> 1) == chip, key, -1)
            low = q & 127
            lhs = jnp.where(key == key_iota, 1.0, 0.0).astype(BF16)
            rhs = jnp.where(low == low_iota, 1.0, 0.0).astype(BF16)
            c = lax.dot_general(lhs, rhs, (((1,), (1,)), ((), ())), preferred_element_type=jnp.float32).astype(BF16)
            at = pl.ds(pl.multiple_of(r * samples, samples), samples)
            for i in range(2 * q_high):
                counts[at, i * 128:(i + 1) * 128] = c[i * samples:(i + 1) * samples]
            return carry

        lax.fori_loop(0, every, one, 0, unroll=UNROLL)
        both = jnp.dot(counts[...], split[...], preferred_element_type=jnp.float32)
        part[t] = (both[:, :columns] + both[:, columns:]).reshape(2, 2, far, pair, columns)

    def step(i, carry):
        ahead = i // per_chunk + 1
        for turn, stage in enumerate((ask_near, ask_last)):
            @pl.when(jnp.logical_and(lax.rem(i, per_chunk) == turn, ahead < chunks))
            def _(stage=stage):
                stage(ahead)

        @pl.when(i < half)
        def _():
            @pl.when(lax.rem(i, per_chunk) == 0)
            def _():
                ask1(i // per_chunk).wait_recv()
                ask12(i // per_chunk).wait_recv()

            split_rows(i)
            product(i)
            first(i).start()

        @pl.when(jnp.logical_and(i >= LAG, i < half + LAG))
        def _():
            t = i - LAG
            first(t).wait_recv()
            part[t, 0, 1] += got1[t, 1]
            second(t).start()
            part[t, 0, 0] += got1[t, 0]

        @pl.when(jnp.logical_and(i >= 2 * LAG, i < half + 2 * LAG))
        def _():
            t = i - 2 * LAG
            second(t).wait_recv()
            part[t, 0, 0] += got2[t]
            for d in range(1, far):
                third(t, d).start()

        @pl.when(jnp.logical_and(i >= 3 * LAG, i < half + 3 * LAG))
        def _():
            t = i - 3 * LAG
            total = part[t, 0, 0, a]
            for d in range(1, far):
                third(t, d).wait_recv()
                total = total + got3[t, d - 1]
            mine[t] = total

        return carry

    lax.fori_loop(0, half + 3 * LAG, step, 0)

    def hand_over(t, carry):
        res[core * half + t] = mine[t, pl.ds(pl.multiple_of(core * samples, samples), samples), :]
        return carry

    last = pltpu.make_async_remote_copy(
        src_ref=mine.at[:, pl.ds(pl.multiple_of((1 - core) * samples, samples), samples), :],
        dst_ref=res.at[pl.ds(core * half, half)],
        send_sem=last_send, recv_sem=last_recv, device_id=sibling, device_id_type=MESH)
    last.start()
    lax.fori_loop(0, half, hand_over, 0)

    def drain(t, carry):
        swap_rows(t).wait_send()
        first(t).wait_send()
        second(t).wait_send()
        for d in range(1, far):
            third(t, d).wait_send()
        return carry

    lax.fori_loop(0, half, drain, 0)
    for k in range(chunks):
        ask0(k).wait_send()
        for d in range(1, far):
            ask3(k, d).wait_send()
        ask2(k).wait_send()
        ask1(k).wait_send()
        ask12(k).wait_send()
    last.wait()
    for c in range(tables):
        out_ref[:, c, :] = res[order_ref[c]]


def body(saved_rows, table_order, owner_shard, row_in_shard, bag_owner):
    groups = lax.axis_size("grp")
    shards = lax.axis_size("row")
    devices = groups * shards
    tables, depth, _, columns = saved_rows.shape
    half = tables // 2
    far = shards // 4
    shard_rows = depth * devices // shards
    ids = owner_shard[:, 0, :, 0] * shard_rows + row_in_shard[:, 0, :]
    chunks = max(1, half // 4)
    per_chunk = half // chunks
    cut = (2, chunks, per_chunk, ids.shape[-1])
    wanted = jnp.concatenate([ids.reshape(cut), bag_owner[:, 0, :].reshape(cut)], axis=2)
    pair = 2 * SAMP_DEV
    f32 = jnp.float32
    dma = pltpu.SemaphoreType.DMA
    return pl.pallas_call(
        functools.partial(pool_kernel, groups, shards),
        out_shape=jax.ShapeDtypeStruct((SAMP_DEV, tables, columns), f32),
        in_specs=[
            pl.BlockSpec(memory_space=pltpu.SMEM),
            pl.BlockSpec(memory_space=pltpu.VMEM),
            pl.BlockSpec(memory_space=pl.ANY),
        ],
        out_specs=pl.BlockSpec(memory_space=pltpu.VMEM),
        scratch_shapes=[
            pltpu.VMEM((chunks, 2, 2, far, 2, 2 * per_chunk, ids.shape[-1]), jnp.int32),
            dma((chunks,)), dma((chunks,)), dma((chunks,)),
            dma((chunks, far - 1)), dma((chunks, far - 1)),
            dma((chunks,)), dma((chunks,)), dma((chunks,)), dma((chunks,)), dma((chunks,)), dma((chunks,)),
            pltpu.VMEM((half, 2, depth, columns), f32),
            pltpu.VMEM((2 * depth, 2 * columns), BF16),
            pltpu.VMEM((4 * far * pair, 2 * depth), BF16),
            pltpu.VMEM((half, 2, 2, far, pair, columns), f32),
            pltpu.VMEM((half, 2, far, pair, columns), f32),
            pltpu.VMEM((half, far, pair, columns), f32),
            pltpu.VMEM((half, far - 1, pair, columns), f32),
            pltpu.VMEM((half, pair, columns), f32),
            pltpu.VMEM((tables, SAMP_DEV, columns), f32),
            dma((half,)), dma((half,)), dma((half,)),
            dma((half,)), dma((half,)), dma((half,)), dma((half,)),
            dma((half, far - 1)), dma((half, far - 1)),
            dma, dma,
        ],
        compiler_params=pltpu.CompilerParams(collective_id=0, has_side_effects=True),
    )(table_order, wanted, saved_rows.reshape(tables, depth, columns))


def solution(mesh):
    return jax.shard_map(
        body,
        mesh=mesh,
        in_specs=(
            P(None, None, ("grp", "row"), None),
            P(),
            P(None, ("grp", "row"), None, None),
            P(None, ("grp", "row"), None),
            P(None, ("grp", "row"), None),
        ),
        out_specs=P(("grp", "row"), None, None),
        check_vma=False,
    )
```

```python
import functools

import jax
import jax.numpy as jnp
from jax import lax
from jax.experimental import pallas as pl
from jax.experimental.pallas import tpu as pltpu
from jax.sharding import PartitionSpec as P

SAMP_DEV = 16
UNROLL = 16
LAG = 2
MESH = pl.DeviceIdType.MESH
BF16 = jnp.bfloat16


def pool_kernel(groups, shards, order_ref, owner_ref, local_ref, bag_ref, saved_ref, out_ref,
                own_ref, ids, own_sem, ask0_send, ask0_recv, ask3_send, ask3_recv, ask4_send, ask4_recv, ask2_send, ask2_recv,
                ask1_send, ask1_recv, ask12_send, ask12_recv,
                rows, split, counts, part, got1, got2, got3, mine, res,
                row_sem, swap_send, swap_recv, send1, recv1, send2, recv2, send3, recv3, last_send, last_recv):
    half, _, depth, columns = rows.shape
    tables = 2 * half
    far = shards // 4
    devices = groups * shards
    assert devices & (devices - 1) == 0
    q_high = depth // 128
    samples = SAMP_DEV
    pair = 2 * samples
    g = lax.axis_index("grp")
    row = lax.axis_index("row")
    core = lax.rem(row, 2)
    m = lax.rem(row // 2, 2)
    a = row // 4
    chip = (g * shards + row) // 2
    flip = 1 - 2 * core

    def place(gg, aa, mm, cc):
        return (gg, (aa * 2 + mm) * 2 + cc)

    sibling = place(g, a, m, 1 - core)
    is0 = 1 - core
    near1 = place(lax.rem(g + is0, 2), a, lax.rem(m + core, 2), core)
    near2 = place(lax.rem(g + core, 2), a, lax.rem(m + is0, 2), core)

    diagonal = place(1 - g, a, 1 - m, core)

    def far_place(d, cc):
        return place(g, lax.rem(a + d, far), m, cc)

    shard_rows = depth * devices // shards
    chunks = ids.shape[0]
    per_chunk = half // chunks
    for t in range(tables):
        h, k, slot = t // half, t % half // per_chunk, t % per_chunk
        own_ref[h, k, slot:slot + 1, :] = owner_ref[t] * shard_rows + local_ref[t]
        own_ref[h, k, per_chunk + slot:per_chunk + slot + 1, :] = bag_ref[t]

    barrier = pltpu.get_barrier_semaphore()
    peers = [sibling, near1, near2, diagonal] + [far_place(d, cc) for d in range(1, far) for cc in (core, 1 - core)]
    for peer in peers:
        pl.semaphore_signal(barrier, inc=1, device_id=peer, device_id_type=MESH)
    pl.semaphore_wait(barrier, len(peers))

    def own_rows(t):
        return pltpu.make_async_copy(saved_ref.at[core * half + t], rows.at[t, core], row_sem.at[t])

    def swap_rows(t):
        return pltpu.make_async_remote_copy(
            src_ref=saved_ref.at[(1 - core) * half + t], dst_ref=rows.at[t, core],
            send_sem=swap_send.at[t], recv_sem=swap_recv.at[t], device_id=sibling, device_id_type=MESH)

    def swap_got(t):
        return pltpu.make_async_remote_copy(
            src_ref=saved_ref.at[(1 - core) * half + t], dst_ref=rows.at[t, 1 - core],
            send_sem=swap_send.at[t], recv_sem=swap_recv.at[t], device_id=sibling, device_id_type=MESH)

    def first(t):
        return pltpu.make_async_remote_copy(
            src_ref=part.at[t, 1], dst_ref=got1.at[t], send_sem=send1.at[t], recv_sem=recv1.at[t],
            device_id=near1, device_id_type=MESH)

    def second(t):
        return pltpu.make_async_remote_copy(
            src_ref=part.at[t, 0, 1], dst_ref=got2.at[t], send_sem=send2.at[t], recv_sem=recv2.at[t],
            device_id=near2, device_id_type=MESH)

    def third(t, d):
        return pltpu.make_async_remote_copy(
            src_ref=part.at[t, 0, 0, lax.rem(a + d, far)], dst_ref=got3.at[t, d - 1],
            send_sem=send3.at[t, d - 1], recv_sem=recv3.at[t, d - 1],
            device_id=far_place(d, core), device_id_type=MESH)

    def start_rows(t, carry):
        own_rows(t).start()
        swap_rows(t).start()
        return carry

    def keep_ids(k):
        return pltpu.make_async_copy(own_ref.at[core, k], ids.at[k, 0, 0, a, core], own_sem.at[k])

    def ask(src, dst, sends, recvs, peer):
        return pltpu.make_async_remote_copy(
            src_ref=src, dst_ref=dst, send_sem=sends, recv_sem=recvs, device_id=peer, device_id_type=MESH)

    def ask0(k):
        return ask(own_ref.at[1 - core, k], ids.at[k, 0, 0, a, core], ask0_send.at[k], ask0_recv.at[k], sibling)

    def ask3(k, d):
        return ask(own_ref.at[core, k], ids.at[k, 0, 0, a, core],
                   ask3_send.at[k, d - 1], ask3_recv.at[k, d - 1], far_place(d, core))

    def ask4(k, d):
        return ask(own_ref.at[1 - core, k], ids.at[k, 0, 0, a, core],
                   ask4_send.at[k, d - 1], ask4_recv.at[k, d - 1], far_place(d, 1 - core))

    def ask2(k):
        return ask(ids.at[k, 0, 0], ids.at[k, 0, 1], ask2_send.at[k], ask2_recv.at[k], near2)

    def ask1(k):
        return ask(ids.at[k, 0, 0], ids.at[k, 1, 0], ask1_send.at[k], ask1_recv.at[k], near1)

    def ask12(k):
        return ask(ids.at[k, 0, 0], ids.at[k, 1, 1], ask12_send.at[k], ask12_recv.at[k], diagonal)

    for k in range(chunks):
        for d in range(1, far):
            ask3(k, d).start()
            ask4(k, d).start()
        ask0(k).start()
        keep_ids(k).start()
    lax.fori_loop(0, half, start_rows, 0)

    def ask_near(k):
        keep_ids(k).wait()
        ask0(k).wait_recv()
        for d in range(1, far):
            ask3(k, d).wait_recv()
            ask4(k, d).wait_recv()
        ask12(k).start()
        ask2(k).start()
        ask1(k).start()

    ask_near(0)

    key_rows = 2 * q_high * samples
    key_iota = lax.broadcasted_iota(jnp.int32, (key_rows, 128), 0)
    low_iota = lax.broadcasted_iota(jnp.int32, (128, 128), 0)

    def split_rows(t):
        own_rows(t).wait()
        swap_got(t).wait_recv()
        for k in range(2):
            x = rows[t, k]
            high = x.astype(BF16)
            split[k * depth:(k + 1) * depth, 0:columns] = high
            split[k * depth:(k + 1) * depth, columns:] = (x - high.astype(jnp.float32)).astype(BF16)

    def product(t):
        every = 2 * 2 * far * 2
        chunk = t // per_chunk
        slot = lax.rem(t, per_chunk)

        def one(r, carry):
            c2 = lax.rem(r, 2)
            aa = lax.rem(r // 2, far)
            p2 = lax.rem(r // (2 * far), 2)
            block = ids.at[chunk, r // (4 * far), p2, aa, c2]
            want = block[pl.ds(slot, 1), :]
            bag = block[pl.ds(per_chunk + slot, 1), :]
            dev = want & (devices - 1)
            q = want >> (devices.bit_length() - 1)
            key = ((dev & 1) * q_high + (q >> 7)) * samples + bag
            key = jnp.where((dev >> 1) == chip, key, -1)
            low = q & 127
            lhs = jnp.where(key == key_iota, 1.0, 0.0).astype(BF16)
            rhs = jnp.where(low == low_iota, 1.0, 0.0).astype(BF16)
            c = lax.dot_general(lhs, rhs, (((1,), (1,)), ((), ())), preferred_element_type=jnp.float32).astype(BF16)
            at = pl.ds(pl.multiple_of(r * samples, samples), samples)
            for i in range(2 * q_high):
                counts[at, i * 128:(i + 1) * 128] = c[i * samples:(i + 1) * samples]
            return carry

        lax.fori_loop(0, every, one, 0, unroll=UNROLL)
        both = jnp.dot(counts[...], split[...], preferred_element_type=jnp.float32)
        part[t] = (both[:, :columns] + both[:, columns:]).reshape(2, 2, far, pair, columns)

    def step(i, carry):
        ahead = i // per_chunk + 1
        @pl.when(jnp.logical_and(lax.rem(i, per_chunk) == 0, ahead < chunks))
        def _():
            ask_near(ahead)

        @pl.when(i < half)
        def _():
            @pl.when(lax.rem(i, per_chunk) == 0)
            def _():
                ask1(i // per_chunk).wait_recv()
                ask2(i // per_chunk).wait_recv()
                ask12(i // per_chunk).wait_recv()

            split_rows(i)
            product(i)
            first(i).start()

        @pl.when(jnp.logical_and(i >= LAG, i < half + LAG))
        def _():
            t = i - LAG
            first(t).wait_recv()
            part[t, 0, 1] += got1[t, 1]
            second(t).start()
            part[t, 0, 0] += got1[t, 0]

        @pl.when(jnp.logical_and(i >= 2 * LAG, i < half + 2 * LAG))
        def _():
            t = i - 2 * LAG
            second(t).wait_recv()
            part[t, 0, 0] += got2[t]
            for d in range(1, far):
                third(t, d).start()

        @pl.when(jnp.logical_and(i >= 3 * LAG, i < half + 3 * LAG))
        def _():
            t = i - 3 * LAG
            total = part[t, 0, 0, a]
            for d in range(1, far):
                third(t, d).wait_recv()
                total = total + got3[t, d - 1]
            mine[t] = total

        return carry

    lax.fori_loop(0, half + 3 * LAG, step, 0)

    def hand_over(t, carry):
        res[core * half + t] = mine[t, pl.ds(pl.multiple_of(core * samples, samples), samples), :]
        return carry

    last = pltpu.make_async_remote_copy(
        src_ref=mine.at[:, pl.ds(pl.multiple_of((1 - core) * samples, samples), samples), :],
        dst_ref=res.at[pl.ds(core * half, half)],
        send_sem=last_send, recv_sem=last_recv, device_id=sibling, device_id_type=MESH)
    last.start()
    lax.fori_loop(0, half, hand_over, 0)

    def drain(t, carry):
        swap_rows(t).wait_send()
        first(t).wait_send()
        second(t).wait_send()
        for d in range(1, far):
            third(t, d).wait_send()
        return carry

    lax.fori_loop(0, half, drain, 0)
    for k in range(chunks):
        ask0(k).wait_send()
        for d in range(1, far):
            ask3(k, d).wait_send()
            ask4(k, d).wait_send()
        ask2(k).wait_send()
        ask1(k).wait_send()
        ask12(k).wait_send()
    last.wait()
    for c in range(tables):
        out_ref[:, c, :] = res[order_ref[c]]


def body(saved_rows, table_order, owner_shard, row_in_shard, bag_owner):
    groups = lax.axis_size("grp")
    shards = lax.axis_size("row")
    devices = groups * shards
    tables, depth, _, columns = saved_rows.shape
    half = tables // 2
    far = shards // 4
    chunks = max(1, half // 4)
    per_chunk = half // chunks
    width = row_in_shard.shape[-1]
    pair = 2 * SAMP_DEV
    f32 = jnp.float32
    dma = pltpu.SemaphoreType.DMA
    return pl.pallas_call(
        functools.partial(pool_kernel, groups, shards),
        out_shape=jax.ShapeDtypeStruct((SAMP_DEV, tables, columns), f32),
        in_specs=[
            pl.BlockSpec(memory_space=pltpu.SMEM),
            pl.BlockSpec(memory_space=pltpu.VMEM),
            pl.BlockSpec(memory_space=pltpu.VMEM),
            pl.BlockSpec(memory_space=pltpu.VMEM),
            pl.BlockSpec(memory_space=pl.ANY),
        ],
        out_specs=pl.BlockSpec(memory_space=pltpu.VMEM),
        scratch_shapes=[
            pltpu.VMEM((2, chunks, 2 * per_chunk, width), jnp.int32),
            pltpu.VMEM((chunks, 2, 2, far, 2, 2 * per_chunk, width), jnp.int32),
            dma((chunks,)), dma((chunks,)), dma((chunks,)),
            dma((chunks, far - 1)), dma((chunks, far - 1)), dma((chunks, far - 1)), dma((chunks, far - 1)),
            dma((chunks,)), dma((chunks,)), dma((chunks,)), dma((chunks,)), dma((chunks,)), dma((chunks,)),
            pltpu.VMEM((half, 2, depth, columns), f32),
            pltpu.VMEM((2 * depth, 2 * columns), BF16),
            pltpu.VMEM((4 * far * pair, 2 * depth), BF16),
            pltpu.VMEM((half, 2, 2, far, pair, columns), f32),
            pltpu.VMEM((half, 2, far, pair, columns), f32),
            pltpu.VMEM((half, far, pair, columns), f32),
            pltpu.VMEM((half, far - 1, pair, columns), f32),
            pltpu.VMEM((half, pair, columns), f32),
            pltpu.VMEM((tables, SAMP_DEV, columns), f32),
            dma((half,)), dma((half,)), dma((half,)),
            dma((half,)), dma((half,)), dma((half,)), dma((half,)),
            dma((half, far - 1)), dma((half, far - 1)),
            dma, dma,
        ],
        compiler_params=pltpu.CompilerParams(collective_id=0, has_side_effects=True),
    )(table_order, owner_shard[..., 0], row_in_shard, bag_owner, saved_rows.reshape(tables, depth, columns))


def solution(mesh):
    return jax.shard_map(
        body,
        mesh=mesh,
        in_specs=(
            P(None, None, ("grp", "row"), None),
            P(),
            P(None, ("grp", "row"), None, None),
            P(None, ("grp", "row"), None),
            P(None, ("grp", "row"), None),
        ),
        out_specs=P(("grp", "row"), None, None),
        check_vma=False,
    )
```
